512 devices in a mesh: pipe: 8 (over y, core), ctx: 16 (over z), head: 4 (over x).
Axes of the slice: x: 4, y: 4, z: 16, core: 2. Of those that a mesh axis runs over, the one named last changes fastest.
Arguments:
- x_in: bfloat16 [8, 12288, 4096], P('pipe', 'ctx', 'head'), may hold values from -6 to 6
- b_in: bfloat16 [8, 12288, 512], P('pipe', 'ctx', 'head'), may hold values from -6 to 6
- c_in: bfloat16 [8, 12288, 512], P('pipe', 'ctx', 'head'), may hold values from -6 to 6
- z_in: bfloat16 [8, 12288, 4096], P('pipe', 'ctx', 'head'), may hold values from -6 to 6
- dt_raw: float32 [8, 12288, 64], P('pipe', 'ctx', 'head'), may hold values from -5 to 5
- seg_ids: int32 [8, 12288], P('pipe', 'ctx'), may hold values from 0 to 3, never falling along the last dimension, each value on 1 to 6144 neighbouring positions
- conv_x: float32 [8, 4, 4096], P('pipe', None, 'head'), may hold values from -3 to 3
- conv_bc: float32 [8, 2, 4, 512], P('pipe', None, None, 'head'), may hold values from -3 to 3
- decay_rate: float32 [8, 64], P('pipe', 'head'), may hold values from 8.138021e-06 to 0.041666667, as said below
- dt_bias: float32 [8, 64], P('pipe', 'head'), may hold values from -1 to 1
- skip_d: float32 [8, 64], P('pipe', 'head'), may hold values from 0.5 to 2
- norm_gain: float32 [8, 4096], P('pipe', 'head'), may hold values from 0.5 to 1.5
Outputs:
- next_rows: bfloat16 [8, 12288, 4096], P('pipe', ('ctx', 'head'))
The draws below stay inside these ranges and needn't reach their ends.
Inputs may be any that keep to these rules, and one draw needn't show every extreme that they name: `seg_ids`: along each section's tokens ids never fall; every request holds 1 to 6144 tokens and one holds exactly 6144. `decay_rate`: positive rates.
All inputs are finite; a program needn't handle non-finite values.
Results may differ from the reference program's by a relative error of at most 0.005.
Values may be sent and summed in bfloat16 or wider, within the bound.
A program may use at most 128 MiB of HBM per device.

```python
import math
import jax
import jax.numpy as jnp
import numpy as np
from jax import lax

HEADS = 64
P_SIZE = 64
N = 128
GROUPS = 4
CONV = 4
SEGS = 4
TOK_DEV = 768
INNER = 4096
GN = 512
TOKENS = 12288
SECTIONS = 8
MOST = 6144
N_CTX = 16


def draw_decay_rate(key, part):
    first_key, second_key, third_key = jax.random.split(key, 3)
    shape = (SECTIONS, HEADS)
    slow = jnp.exp(jax.random.uniform(first_key, shape, jnp.float32, math.log(0.11 / TOKENS), math.log(1.0 / TOKENS)))
    fast = jnp.exp(jax.random.uniform(second_key, shape, jnp.float32, math.log(1.0 / TOKENS), math.log(1.0 / 25.0)))
    picker = jax.random.uniform(third_key, shape, jnp.float32)
    share = 0.5
    return jnp.where(picker < share, fast, slow)


def block_levels(rng, extent, cuts, least, high):
    level = 1.0
    for dim, blocks in cuts:
        steps = jax.random.uniform(jax.random.fold_in(jax.random.fold_in(rng, 6), dim), (blocks,), jnp.float32, least / len(cuts), high / len(cuts))
        level = level * jnp.repeat(jnp.exp(steps), extent[dim] // blocks).reshape((-1,) + (1,) * (len(extent) - 1 - dim))
    return level


def split_up(number_of, total, most, slope):
    weights = [(1 << 20) // math.isqrt(grade ** slope) + 1 for grade in range(2, number_of + 1)]
    spare, given = total - most - (number_of - 1), [1] * (number_of - 1)
    while spare > 0:
        free = [i for i in range(number_of - 1) if given[i] < most]
        mass, budget = sum([weights[i] for i in free]), spare
        for i in free:
            extra = min(most - given[i], max(1, budget * weights[i] // mass), spare)
            given[i] = given[i] + extra
            spare = spare - extra
    return np.array([most] + given)


def ragged_sizes(stream_key, count, total, reach, lean):
    if count == 2:
        one = jax.random.randint(stream_key, (), max(1, total - reach), min(reach, total - 1) + 1)
        return jnp.stack([one, total - one])
    sizes = jnp.asarray(split_up(count, total, reach, lean), jnp.int32)
    couples = (count - 1) // 2
    source_of, sink = sizes[1:1 + 2 * couples:2], sizes[2:2 + 2 * couples:2]
    room = jnp.minimum(source_of - 1, reach - sink)
    moved = jax.random.randint(jax.random.fold_in(stream_key, 1), (couples,), 0, 1 << 20) % (room + 1)
    sizes = sizes.at[1:1 + 2 * couples:2].set(source_of - moved).at[2:2 + 2 * couples:2].set(sink + moved)
    return sizes[jax.random.permutation(jax.random.fold_in(stream_key, 2), count)]


def noise(rng, dims, scale, most, pieces=(), kind=jnp.bfloat16):
    gain = block_levels(rng, dims, pieces, -0.22, 0.18) if pieces else 1.0
    drawn = jax.random.normal(rng, dims, jnp.float32) * scale * gain
    return jnp.minimum(jnp.maximum(drawn, -most), most).astype(kind)


def setup_inputs(seed: int = 0) -> dict:
    key_list = jax.random.split(jax.random.key(seed), 13)
    return {
        "x_in": noise(key_list[0], (SECTIONS, TOKENS, INNER), 1.0, 6.0, ((0, 8), (1, 16), (2, 4))),
        "b_in": noise(key_list[1], (SECTIONS, TOKENS, GN), 1.0, 6.0, ((0, 8), (1, 16), (2, 4))),
        "c_in": noise(key_list[2], (SECTIONS, TOKENS, GN), 1.0, 6.0, ((0, 8), (1, 16), (2, 4))),
        "z_in": noise(key_list[3], (SECTIONS, TOKENS, INNER), 1.0, 6.0, ((0, 8), (1, 16), (2, 4))),
        "dt_raw": noise(key_list[4], (SECTIONS, TOKENS, HEADS), 1.0, 5.0, ((0, 8), (1, 16), (2, 4)), jnp.float32),
        "seg_ids": jax.vmap(lambda own: jnp.searchsorted(jnp.cumsum(ragged_sizes(own, SEGS, TOKENS, MOST, 2)), jnp.arange(TOKENS), side="right"))(jax.random.split(key_list[5], SECTIONS)).reshape((SECTIONS, TOKENS)).astype(jnp.int32),
        "conv_x": noise(key_list[6], (SECTIONS, CONV, INNER), CONV ** -0.5, 3.0, ((0, 8), (2, 4)), jnp.float32),
        "conv_bc": noise(key_list[7], (SECTIONS, 2, CONV, GN), CONV ** -0.5, 3.0, ((0, 8), (3, 4)), jnp.float32),
        "decay_rate": draw_decay_rate(jax.random.fold_in(key_list[12], 71), 0),
        "dt_bias": jnp.clip(jax.random.uniform(key_list[9], (SECTIONS, HEADS), jnp.float32, -1.0, 1.0) * block_levels(key_list[9], (SECTIONS, HEADS), ((0, 8), (1, 4)), -0.4, 0.0), -1.0, 1.0),
        "skip_d": jnp.clip(0.5 + 1.5 * jax.random.uniform(key_list[10], (SECTIONS, HEADS), jnp.float32) ** block_levels(key_list[10], (SECTIONS, HEADS), ((0, 8), (1, 4)), -0.2, 0.2), 0.5, 2.0),
        "norm_gain": jnp.clip(1.0 + 0.1 * jax.random.normal(key_list[11], (SECTIONS, INNER), jnp.float32), 0.5, 1.5),
    }


def conv_silu(current, previous, kernel, segments, prev_segments):
    length = current.shape[0]
    extended = jnp.concatenate([previous, current], axis=0)
    ext_segments = jnp.concatenate([prev_segments, segments], axis=0)
    total = jnp.zeros(current.shape, jnp.float32)
    for offset in range(kernel.shape[0]):
        same = (ext_segments[offset:offset + length] == segments)[:, None]
        total = total + jnp.where(same, kernel[offset] * extended[offset:offset + length], 0.0)
    return jax.nn.silu(total).astype(jnp.bfloat16)

def one_section(items):
    values, key_rows, query_rows, gate_rows, raw_steps, segments, taps_x, taps_bc, rates, biases, skips, gains = items
    margin = CONV - 1
    zero_pad = jnp.zeros((margin, values.shape[1]), values.dtype)
    zero_small = jnp.zeros((margin, key_rows.shape[1]), key_rows.dtype)
    seg_pad = jnp.full((margin,), -1, jnp.int32)
    mixed_x = conv_silu(values, zero_pad, taps_x, segments, seg_pad)
    mixed_b = conv_silu(key_rows, zero_small, taps_bc[0], segments, seg_pad)
    mixed_c = conv_silu(query_rows, zero_small, taps_bc[1], segments, seg_pad)
    steps_dt = jax.nn.softplus(raw_steps + biases[None, :])
    log_decay = -steps_dt * rates[None, :]
    per_group = HEADS // GROUPS
    blocks = (mixed_x.reshape(N_CTX, TOK_DEV, HEADS * P_SIZE), mixed_b.reshape(N_CTX, TOK_DEV, GN), mixed_c.reshape(N_CTX, TOK_DEV, GN), segments.reshape(N_CTX, TOK_DEV), steps_dt.reshape(N_CTX, TOK_DEV, HEADS), log_decay.reshape(N_CTX, TOK_DEV, HEADS))
    position = jnp.arange(TOK_DEV)

    def block_step(carry, item):
        state, prior = carry
        block_x, block_b, block_c, block_seg, block_dt, block_log = item
        cum = jnp.cumsum(block_log, axis=0)
        last = block_seg[TOK_DEV - 1]
        head_x = block_x.reshape(TOK_DEV, HEADS, P_SIZE)
        group_b = block_b.reshape(TOK_DEV, GROUPS, N)
        group_c = block_c.reshape(TOK_DEV, GROUPS, N)
        scores = jnp.einsum('tgn,sgn->gts', group_c.astype(jnp.float32), group_b.astype(jnp.float32))
        head_scores = jnp.repeat(scores, per_group, axis=0)
        causal = (position[:, None] >= position[None, :]) & (block_seg[:, None] == block_seg[None, :])
        cum_t = cum.T
        gap = jnp.where(causal[None], cum_t[:, :, None] - cum_t[:, None, :], 0.0)
        weights = jnp.where(causal[None], head_scores * jnp.exp(gap) * block_dt.T[:, None, :], 0.0).astype(jnp.bfloat16)
        intra = jnp.einsum('hts,shp->thp', weights.astype(jnp.float32), head_x.astype(jnp.float32))
        tail = jnp.exp(cum[TOK_DEV - 1][None, :] - cum) * block_dt * (block_seg == last).astype(jnp.float32)[:, None]
        scaled = (head_x * tail[:, :, None]).astype(jnp.bfloat16)
        local = jnp.einsum('sgkp,sgn->gkpn', scaled.reshape(TOK_DEV, GROUPS, per_group, P_SIZE).astype(jnp.float32), group_b.astype(jnp.float32)).reshape(HEADS, P_SIZE, N)
        inter = jnp.einsum('tgn,gkpn->tgkp', group_c.astype(jnp.float32), state.reshape(GROUPS, per_group, P_SIZE, N), precision=lax.Precision.HIGHEST).reshape(TOK_DEV, HEADS, P_SIZE)
        entry = jnp.exp(cum) * (block_seg == prior).astype(jnp.float32)[:, None]
        mixed = intra + entry[:, :, None] * inter + skips[None, :, None] * head_x
        through = jnp.exp(cum[TOK_DEV - 1]) * (last == prior).astype(jnp.float32)
        new_state = through[:, None, None] * state + local
        return ((new_state, last), mixed)
    start = (jnp.zeros((HEADS, P_SIZE, N), jnp.float32), jnp.array(-1, jnp.int32))
    _, mixed_all = lax.scan(block_step, start, blocks)
    gated = mixed_all.reshape(TOKENS, HEADS * P_SIZE) * jax.nn.silu(gate_rows.astype(jnp.float32))
    grouped = gated.reshape(TOKENS, GROUPS, HEADS * P_SIZE // GROUPS)
    stats = lax.optimization_barrier(jnp.mean(grouped * grouped, axis=-1, keepdims=True))
    normed = (grouped * lax.rsqrt(stats + 1e-05)).reshape(TOKENS, HEADS * P_SIZE)
    return (normed * gains[None, :]).astype(jnp.bfloat16)

def reference(x_in, b_in, c_in, z_in, dt_raw, seg_ids, conv_x, conv_bc, decay_rate, dt_bias, skip_d, norm_gain):
    section_out = lax.map(one_section, (x_in, b_in, c_in, z_in, dt_raw, seg_ids, conv_x, conv_bc, decay_rate, dt_bias, skip_d, norm_gain))
    return jnp.roll(section_out, 1, axis=0)
```

```python
import functools

import jax
import jax.numpy as jnp
from jax import lax
from jax.experimental import pallas as pl
from jax.experimental.pallas import tpu as pltpu
from jax.sharding import PartitionSpec as P

F32 = jnp.float32
BF16 = jnp.bfloat16
MESH = pl.DeviceIdType.MESH
CHUNK = 256
LANES = 128
MARGIN = 16
GROUP = 4
HI = lax.Precision.HIGHEST


def nt(a, b, **kw):
    return lax.dot_general(a, b, (((1,), (1,)), ((), ())), preferred_element_type=F32, **kw)


def nn(a, b, **kw):
    return lax.dot_general(a, b, (((1,), (0,)), ((), ())), preferred_element_type=F32, **kw)


def halves(a):
    high = a.astype(BF16)
    return high, (a - high.astype(F32)).astype(BF16)


def silu(a):
    half = 0.5 * a
    return half + half * jnp.tanh(half)


def column(row):
    return jnp.broadcast_to(row, (LANES, LANES)).T


def kernel(
    sizes,
    x_hbm, b_hbm, c_hbm, z_hbm, dt_ref, seg_hbm, conv_x, conv_bc, rate_ref, bias_ref, skip_ref, gain_ref,
    out_hbm,
    xv, bv, cv, zv, segv, mx, mb, mc, mseg, ext, segc, taps, fin, fout, ent, spread, rows_s, bmt, smask, cs, cmask,
    xs, xsc, hid, yg, eg, ssq, chain_in, chain_out, exch_in, relay_in, relay_out, sendbuf, recvbuf, scale_out, scale_in,
    stage,
    load_sem, marg_send, marg_recv, ch_send, ch_recv, ex_send, ex_recv, re_send, re_recv, o_send, o_recv, s_send, s_recv,
    out_sem,
):
    n_pipe, n_ctx, n_head = sizes
    tokens, width = x_hbm.shape
    pieces, chunks = width // LANES, tokens // CHUNK
    heads = rate_ref.shape[1]
    share = tokens // n_head
    sec, blk, me = lax.axis_index("pipe"), lax.axis_index("ctx"), lax.axis_index("head")
    group, place = blk // GROUP, lax.rem(blk, GROUP)
    dest_sec = lax.rem(sec + 1, n_pipe)

    loads = []
    for p in range(pieces):
        loads.append(pltpu.make_async_copy(x_hbm.at[:, pl.ds(p * LANES, LANES)], xv.at[p], load_sem.at[p]))
    for n, (src, dst) in enumerate(((b_hbm, bv), (c_hbm, cv), (z_hbm, zv), (seg_hbm, segv))):
        loads.append(pltpu.make_async_copy(src, dst, load_sem.at[pieces + n]))
    for copy in reversed(loads):
        copy.start()

    barrier = pltpu.get_barrier_semaphore()
    count = 0
    for step in (1, GROUP):
        for peer in (blk + step, blk + n_ctx - step):
            pl.semaphore_signal(barrier, inc=1, device_id={"ctx": lax.rem(peer, n_ctx)}, device_id_type=MESH)
            count += 1
    for peer in (dest_sec, lax.rem(sec + n_pipe - 1, n_pipe)):
        for h in range(n_head):
            pl.semaphore_signal(barrier, inc=1, device_id={"pipe": peer, "head": h}, device_id_type=MESH)
            count += 1
    pl.semaphore_wait(barrier, count)

    nxt = {"ctx": lax.rem(blk + 1, n_ctx)}
    far = {"ctx": lax.rem(blk + GROUP, n_ctx)}

    def remote(src, dst, send, recv, device):
        return pltpu.make_async_remote_copy(
            src_ref=src, dst_ref=dst, send_sem=send, recv_sem=recv, device_id=device, device_id_type=MESH
        )

    margins = [
        remote(b_hbm.at[pl.ds(tokens - MARGIN, MARGIN), :], mb, marg_send.at[0], marg_recv.at[0], nxt),
        remote(c_hbm.at[pl.ds(tokens - MARGIN, MARGIN), :], mc, marg_send.at[1], marg_recv.at[1], nxt),
        remote(seg_hbm.at[:, pl.ds(tokens - LANES, LANES)], mseg, marg_send.at[2], marg_recv.at[2], nxt),
        remote(x_hbm.at[pl.ds(tokens - MARGIN, MARGIN), :], mx, marg_send.at[3], marg_recv.at[3], nxt),
    ]

    @pl.when(blk < n_ctx - 1)
    def _():
        for copy in margins:
            copy.start()

    def chain_copy(p):
        return remote(chain_out.at[p], chain_in.at[p], ch_send.at[p], ch_recv.at[p], nxt)

    def exch_copy(p):
        return remote(chain_in.at[p, pl.ds(0, LANES), :], exch_in.at[p], ex_send.at[p], ex_recv.at[p], far)

    def relay_copy(p):
        return remote(relay_out.at[p], relay_in.at[p], re_send.at[p], re_recv.at[p], nxt)

    def relay_on(p):
        return remote(relay_in.at[p], relay_in.at[p], re_send.at[p], re_recv.at[p], nxt)

    def row_copy(p, d):
        return remote(
            sendbuf.at[p, pl.ds(d * share, share), :],
            recvbuf.at[me, p],
            o_send.at[d, p],
            o_recv.at[me, p],
            {"pipe": dest_sec, "head": d},
        )

    def row_wait(p, h):
        remote(
            sendbuf.at[p, pl.ds(0, share), :], recvbuf.at[h, p], o_send.at[0, p], o_recv.at[h, p],
            {"pipe": dest_sec, "head": 0},
        ).wait_recv()

    def scale_copy(d):
        return remote(scale_out.at[d], scale_in.at[me], s_send.at[d], s_recv.at[me], {"pipe": dest_sec, "head": d})

    def scale_wait(h):
        remote(
            scale_out.at[0], scale_in.at[h], s_send.at[0], s_recv.at[h], {"pipe": dest_sec, "head": 0}
        ).wait_recv()

    loads[pieces + 3].wait()
    eye = lax.broadcasted_iota(jnp.int32, (heads, heads), 0) == lax.broadcasted_iota(jnp.int32, (heads, heads), 1)
    bias = jnp.sum(jnp.where(eye, bias_ref[...], 0.0), axis=1, keepdims=True)
    rate = jnp.sum(jnp.where(eye, rate_ref[...], 0.0), axis=1, keepdims=True)
    raw = dt_ref[...] + bias
    steps = jnp.maximum(raw, 0.0) + jnp.log1p(jnp.exp(-jnp.abs(raw)))
    decay = -steps * rate
    at = lax.broadcasted_iota(jnp.int32, (CHUNK, CHUNK), 0)
    of = lax.broadcasted_iota(jnp.int32, (CHUNK, CHUNK), 1)
    lower = (at >= of).astype(F32)
    unit = (at == of).astype(F32)
    for p in range(pieces):
        head_of = lax.broadcasted_iota(jnp.int32, (heads, LANES), 0)
        lane = lax.broadcasted_iota(jnp.int32, (heads, LANES), 1)
        spread[p] = (head_of == p * (heads // pieces) + lane // (LANES // (heads // pieces))).astype(BF16)

    for n in range(tokens // LANES):
        segc[pl.ds(MARGIN + n * LANES, LANES), :] = column(segv[:, pl.ds(n * LANES, LANES)].astype(F32))

    @pl.when(blk == 0)
    def _():
        mx[...] = jnp.zeros_like(mx)
        mb[...] = jnp.zeros_like(mb)
        mc[...] = jnp.zeros_like(mc)
        mseg[...] = jnp.full_like(mseg, -1)

    @pl.when(blk > 0)
    def _():
        for copy in margins[:3]:
            copy.wait_recv()

    segc[pl.ds(0, MARGIN), :] = column(mseg[...].astype(F32))[LANES - MARGIN :, :]
    for j in range(1, 4):
        for r in range(0, tokens, LANES):
            same = segc[pl.ds(MARGIN + r - j, LANES), :] == segc[pl.ds(MARGIN + r, LANES), :]
            taps[j - 1, pl.ds(r, LANES), :] = same.astype(F32)
    prior = segc[pl.ds(MARGIN - 1, 1), :]
    lasts = [segc[pl.ds(MARGIN + (j + 1) * CHUNK - 1, 1), :] for j in range(chunks)]

    base = jnp.zeros((1, heads), F32)
    rows = []
    for j in range(chunks):
        span = pl.ds(j * CHUNK, CHUNK)
        cum = nt(lower, decay[:, j * CHUNK : (j + 1) * CHUNK], precision=HI)
        step = nt(unit, steps[:, j * CHUNK : (j + 1) * CHUNK], precision=HI)
        last_cum = cum[CHUNK - 1 :, :]
        fin[0, span, :], fin[1, span, :] = halves(jnp.exp(-cum) * step)
        fout[0, span, :], fout[1, span, :] = halves(jnp.exp(cum))
        here = segc[pl.ds(MARGIN + j * CHUNK, CHUNK), :][:, :heads] == prior[:, :heads]
        ent[0, span, :], ent[1, span, :] = halves(jnp.where(here, jnp.exp(cum + base), 0.0))
        base = base + last_cum
        rows.append(jnp.exp(last_cum))
        if j > 0:
            rows.append(jnp.where((lasts[j] == lasts[j - 1])[:, :heads], rows[-1], 0.0))
    rows.append(jnp.where((lasts[-1] == prior)[:, :heads], jnp.exp(base), 0.0))
    rows.append(skip_ref[...])
    rows.append(jnp.zeros((16 - len(rows), heads), F32))
    rows_s[0], rows_s[1] = halves(jnp.concatenate(rows, axis=0))

    def convolved(get, put):
        pass

    def conv_rows(w, r, size):
        total = w[3:4, :] * ext[pl.ds(MARGIN + r, size), :]
        for j in range(1, 4):
            shifted = ext[pl.ds(MARGIN + r - j, size), :]
            total = total + (w[3 - j : 4 - j, :] * shifted) * taps[j - 1, pl.ds(r, size), :]
        return silu(total)

    part = 64
    loads[pieces].wait()
    ext[pl.ds(0, MARGIN), :] = mb[...].astype(F32)
    ext[pl.ds(MARGIN, tokens), :] = bv[...].astype(F32)
    for r in range(0, tokens, part):
        bv[pl.ds(r, part), :] = conv_rows(conv_bc[0], r, part).astype(BF16)
    loads[pieces + 1].wait()
    ext[pl.ds(0, MARGIN), :] = mc[...].astype(F32)
    ext[pl.ds(MARGIN, tokens), :] = cv[...].astype(F32)
    for r in range(0, tokens, part):
        cs[pl.ds(r, part), :] = conv_rows(conv_bc[1], r, part).astype(BF16)
    for j in range(chunks):
        seg_t = segc[pl.ds(MARGIN + j * CHUNK, CHUNK), :]
        state_in = bv[pl.ds(j * CHUNK, CHUNK), :]
        kept = jnp.where(seg_t == lasts[j], state_in.astype(F32), 0.0)
        bmt[j] = kept.T.astype(BF16)

    @pl.when(blk > 0)
    def _():
        margins[3].wait_recv()

    def expand(pair, span, p):
        return nn(pair[0, span, :], spread[p]) + nn(pair[1, span, :], spread[p])

    @pl.loop(0, pieces)
    def _(p):
        lanes = pl.ds(pl.multiple_of(p * LANES, LANES), LANES)
        pltpu.make_async_copy(x_hbm.at[:, lanes], xv.at[p], load_sem.at[p]).wait()
        ext[pl.ds(0, MARGIN), :] = mx[:, lanes].astype(F32)
        ext[pl.ds(MARGIN, tokens), :] = xv[p].astype(F32)
        w = conv_x[:, lanes]
        factors = expand(rows_s, pl.ds(0, 16), p)
        state, row = None, 0
        for j in range(chunks):
            for r in range(j * CHUNK, (j + 1) * CHUNK, part):
                span = pl.ds(r, part)
                value = conv_rows(w, r, part).astype(BF16)
                xs[p, span, :] = value
                xsc[p, span, :] = (value.astype(F32) * expand(fin, span, p)).astype(BF16)
            own = nn(bmt[j], xsc[p, pl.ds(j * CHUNK, CHUNK), :])
            if j == 0:
                state = factors[row : row + 1, :] * own
                row += 1
            else:
                hid[p, j - 1] = state.astype(BF16)
                state = factors[row + 1 : row + 2, :] * state + factors[row : row + 1, :] * own
                row += 2
        through = factors[row : row + 1, :]

        @pl.when(place == 0)
        def _():
            chain_out[p, pl.ds(0, LANES), :] = state.astype(BF16)
            high, low = halves(through)
            chain_out[p, pl.ds(LANES, 16), :] = jnp.concatenate(
                [high, low, jnp.zeros((14, LANES), BF16)], axis=0
            )

        @pl.when(place > 0)
        def _():
            chain_copy(p).wait_recv()
            tail = chain_in[p, pl.ds(LANES, 16), :].astype(F32)
            so_far = tail[0:1, :] + tail[1:2, :]
            chain_out[p, pl.ds(0, LANES), :] = (
                state + through * chain_in[p, pl.ds(0, LANES), :].astype(F32)
            ).astype(BF16)
            high, low = halves(through * so_far)
            chain_out[p, pl.ds(LANES, 16), :] = jnp.concatenate(
                [high, low, jnp.zeros((14, LANES), BF16)], axis=0
            )

        @pl.when(blk < n_ctx - 1)
        def _():
            chain_copy(p).start()

    for j in range(chunks):
        span = pl.ds(j * CHUNK, CHUNK)
        seg_t = segc[pl.ds(MARGIN + j * CHUNK, CHUNK), :]
        for half in range(0, CHUNK, LANES):
            seg_u = segv[:, pl.ds(j * CHUNK + half, LANES)].astype(F32)
            score = nt(cs[span, :], bv[pl.ds(j * CHUNK + half, LANES), :])
            keep = (seg_t == seg_u) & (at[:, :LANES] >= of[:, :LANES] + half)
            smask[j, :, pl.ds(half, LANES)] = jnp.where(keep, score, 0.0).astype(BF16)
        if j > 0:
            kept = jnp.where(seg_t == lasts[j - 1], cs[span, :].astype(F32), 0.0)
            cmask[j - 1] = kept.astype(BF16)
    loads[pieces + 2].wait()

    @pl.loop(0, pieces)
    def _(p):
        lanes = pl.ds(pl.multiple_of(p * LANES, LANES), LANES)
        factors = expand(rows_s, pl.ds(0, 16), p)
        skip = factors[2 * chunks : 2 * chunks + 1, :]
        for j in range(chunks):
            inner = nn(smask[j], xsc[p, pl.ds(j * CHUNK, CHUNK), :])
            if j > 0:
                inner = inner + nn(cmask[j - 1], hid[p, j - 1])
            for r in range(0, CHUNK, part):
                span = pl.ds(j * CHUNK + r, part)
                gate = silu(zv[span, lanes].astype(F32))
                mixed = expand(fout, span, p) * inner[r : r + part, :] + skip * xs[p, span, :].astype(F32)
                yg[p, span, :] = mixed * gate
                eg[p, span, :] = expand(ent, span, p) * gate

        @pl.when((place == 0) & (group > 0))
        def _():
            chain_copy(p).wait_recv()

        @pl.when((place == 0) & (group > 0) & (blk + GROUP < n_ctx))
        def _():
            exch_copy(p).start()

    ssq[...] = jnp.zeros_like(ssq)
    scale_out[...] = jnp.zeros_like(scale_out)

    @pl.loop(0, pieces)
    def _(p):
        lanes = pl.ds(pl.multiple_of(p * LANES, LANES), LANES)

        @pl.when(blk == 0)
        def _():
            relay_out[p] = jnp.zeros((LANES, LANES), BF16)

        @pl.when((place == 0) & (group == 1))
        def _():
            relay_out[p] = chain_in[p, pl.ds(0, LANES), :]

        @pl.when((place == 0) & (group > 1))
        def _():
            exch_copy(p).wait_recv()
            tail = chain_in[p, pl.ds(LANES, 16), :].astype(F32)
            so_far = tail[0:1, :] + tail[1:2, :]
            relay_out[p] = (
                chain_in[p, pl.ds(0, LANES), :].astype(F32) + so_far * exch_in[p].astype(F32)
            ).astype(BF16)

        @pl.when((place == 0) & (group > 0))
        def _():
            relay_copy(p).start()

        @pl.when((place > 0) & (group == 0))
        def _():
            relay_out[p] = chain_in[p, pl.ds(0, LANES), :]

        @pl.when((place > 0) & (group > 0))
        def _():
            relay_on(p).wait_recv()

        @pl.when((place > 0) & (place < GROUP - 1) & (group > 0))
        def _():
            relay_on(p).start()

        @pl.when((place > 0) & (group > 0))
        def _():
            tail = chain_in[p, pl.ds(LANES, 16), :].astype(F32)
            so_far = tail[0:1, :] + tail[1:2, :]
            relay_out[p] = (
                chain_in[p, pl.ds(0, LANES), :].astype(F32) + so_far * relay_in[p].astype(F32)
            ).astype(BF16)

        gain = gain_ref[:, lanes]
        for r in range(0, tokens, part):
            span = pl.ds(r, part)
            gated = yg[p, span, :] + eg[p, span, :] * nn(cs[span, :], relay_out[p])
            ssq[span, :] += gated * gated
            sendbuf[p, span, :] = (gated * gain).astype(BF16)
        for turn in range(n_head):
            row_copy(p, lax.rem(me + turn, n_head)).start()

    for d in range(n_head):
        for n, first in enumerate((0, share - LANES)):
            total = jnp.sum(ssq[pl.ds(d * share + first, LANES), :].T, axis=0, keepdims=True)
            scale_out[d, pl.ds(n, 1), :] = lax.rsqrt(total * (1.0 / width) + 1e-05)
        scale_copy(d).start()

    for h in range(n_head):
        scale_wait(h)
        first = column(scale_in[h, pl.ds(0, 1), :])
        second = column(scale_in[h, pl.ds(1, 1), :])

        @pl.loop(0, pieces)
        def _(p):
            row_wait(p, h)
            lanes = pl.ds(pl.multiple_of(h * width + p * LANES, LANES), LANES)
            stage[pl.ds(0, LANES), lanes] = (recvbuf[h, p, pl.ds(0, LANES), :].astype(F32) * first).astype(BF16)
            rest = share - LANES
            stage[pl.ds(LANES, rest), lanes] = (
                recvbuf[h, p, pl.ds(LANES, rest), :].astype(F32) * second[LANES - rest :, :]
            ).astype(BF16)

        pltpu.make_async_copy(
            stage.at[:, pl.ds(h * width, width)], out_hbm.at[:, pl.ds(h * width, width)], out_sem.at[h]
        ).start()

    for h in range(n_head):
        pltpu.make_async_copy(
            stage.at[:, pl.ds(h * width, width)], out_hbm.at[:, pl.ds(h * width, width)], out_sem.at[h]
        ).wait()
    for d in range(n_head):
        scale_copy(d).wait_send()

    @pl.loop(0, pieces)
    def _(p):
        for d in range(n_head):
            row_copy(p, d).wait_send()

        @pl.when(blk < n_ctx - 1)
        def _():
            chain_copy(p).wait_send()

        @pl.when((place == 0) & (group > 0) & (blk + GROUP < n_ctx))
        def _():
            exch_copy(p).wait_send()

        @pl.when((place < GROUP - 1) & (group > 0))
        def _():
            relay_copy(p).wait_send()

    @pl.when(blk < n_ctx - 1)
    def _():
        for copy in margins:
            copy.wait_send()


def solution(mesh):
    sizes = tuple(mesh.shape[name] for name in ("pipe", "ctx", "head"))
    n_head = sizes[2]

    def shards(
        x_in, b_in, c_in, z_in, dt_raw, seg_ids, conv_x, conv_bc, decay_rate, dt_bias, skip_d, norm_gain
    ):
        _, tokens, width = x_in.shape
        state = b_in.shape[2]
        heads = decay_rate.shape[1]
        pieces, chunks, share = width // LANES, tokens // CHUNK, tokens // n_head
        vmem, sem = pltpu.VMEM, pltpu.SemaphoreType.DMA
        scratch = [
            vmem((pieces, tokens, LANES), BF16),
            vmem((tokens, state), BF16),
            vmem((tokens, state), BF16),
            vmem((tokens, width), BF16),
            vmem((1, tokens), jnp.int32),
            vmem((MARGIN, width), BF16),
            vmem((MARGIN, state), BF16),
            vmem((MARGIN, state), BF16),
            vmem((1, LANES), jnp.int32),
            vmem((MARGIN + tokens, LANES), F32),
            vmem((MARGIN + tokens, LANES), F32),
            vmem((3, tokens, LANES), F32),
            vmem((2, tokens, heads), BF16),
            vmem((2, tokens, heads), BF16),
            vmem((2, tokens, heads), BF16),
            vmem((pieces, heads, LANES), BF16),
            vmem((2, 16, heads), BF16),
            vmem((chunks, state, CHUNK), BF16),
            vmem((chunks, CHUNK, CHUNK), BF16),
            vmem((tokens, state), BF16),
            vmem((chunks - 1, CHUNK, state), BF16),
            vmem((pieces, tokens, LANES), BF16),
            vmem((pieces, tokens, LANES), BF16),
            vmem((pieces, chunks - 1, state, LANES), BF16),
            vmem((pieces, tokens, LANES), F32),
            vmem((pieces, tokens, LANES), F32),
            vmem((tokens, LANES), F32),
            vmem((pieces, state + 16, LANES), BF16),
            vmem((pieces, state + 16, LANES), BF16),
            vmem((pieces, state, LANES), BF16),
            vmem((pieces, state, LANES), BF16),
            vmem((pieces, state, LANES), BF16),
            vmem((pieces, tokens, LANES), BF16),
            vmem((n_head, pieces, share, LANES), BF16),
            vmem((n_head, 8, LANES), F32),
            vmem((n_head, 8, LANES), F32),
            vmem((share, n_head * width), BF16),
            sem((pieces + 4,)),
            sem((4,)), sem((4,)),
            sem((pieces,)), sem((pieces,)),
            sem((pieces,)), sem((pieces,)),
            sem((pieces,)), sem((pieces,)),
            sem((n_head, pieces)), sem((n_head, pieces)),
            sem((n_head,)), sem((n_head,)),
            sem((n_head,)),
        ]
        anywhere = pl.BlockSpec(memory_space=pl.ANY)
        local = pl.BlockSpec(memory_space=pltpu.VMEM)
        rows = pl.pallas_call(
            functools.partial(kernel, sizes),
            out_shape=jax.ShapeDtypeStruct((share, n_head * width), BF16),
            in_specs=[anywhere] * 4 + [local, anywhere] + [local] * 6,
            out_specs=anywhere,
            scratch_shapes=scratch,
            compiler_params=pltpu.CompilerParams(collective_id=0, has_side_effects=True),
        )(
            x_in[0], b_in[0], c_in[0], z_in[0], dt_raw[0].T, seg_ids, conv_x[0], conv_bc[0],
            decay_rate, dt_bias, skip_d, norm_gain,
        )
        return rows[None]

    placed = (
        P("pipe", "ctx", "head"),
        P("pipe", "ctx", "head"),
        P("pipe", "ctx", "head"),
        P("pipe", "ctx", "head"),
        P("pipe", "ctx", "head"),
        P("pipe", "ctx"),
        P("pipe", None, "head"),
        P("pipe", None, None, "head"),
        P("pipe", "head"),
        P("pipe", "head"),
        P("pipe", "head"),
        P("pipe", "head"),
    )
    return jax.shard_map(
        shards,
        mesh=mesh,
        in_specs=placed,
        out_specs=P("pipe", ("ctx", "head"), None),
        check_vma=False,
    )
```

```python
import functools

import jax
import jax.numpy as jnp
from jax import lax
from jax.experimental import pallas as pl
from jax.experimental.pallas import tpu as pltpu
from jax.sharding import PartitionSpec as P

F32 = jnp.float32
BF16 = jnp.bfloat16
MESH = pl.DeviceIdType.MESH
CHUNK = 256
LANES = 128
MARGIN = 16
HALF = 64


def nt(a, b, **kw):
    return lax.dot_general(a, b, (((1,), (1,)), ((), ())), preferred_element_type=F32, **kw)


def nn(a, b, **kw):
    return lax.dot_general(a, b, (((1,), (0,)), ((), ())), preferred_element_type=F32, **kw)


def halves(a):
    high = a.astype(BF16)
    return high, (a - high.astype(F32)).astype(BF16)


def silu(a):
    half = 0.5 * a
    return half + half * jnp.tanh(half)


def column(row):
    return jnp.broadcast_to(row, (LANES, LANES)).T


def kernel(
    sizes,
    x_hbm, b_hbm, c_hbm, z_hbm, dt_hbm, seg_hbm, convx_hbm, convbc_hbm, rate_hbm, bias_hbm, skip_hbm, gain_hbm,
    recvbuf, scale_in,
    xv, bv, cv, zv, dtv, segv, conv_x, conv_bc, ratev, biasv, skipv, gainv, mx, mb, mc, mseg,
    ext, segc, taps, fac, spread_in, spread_out, rows_s, bmt, smask, cs, cmask,
    xs, xsc, hid, yg, eg, ssq, loc_out, t_out, loc_in, t_in, scan_s, c_out, c_in, car, sendbuf, scale_out,
    load_sem, small_sem, marg_send, marg_recv, l_send, l_recv, t_send, t_recv, c_send, c_recv,
    o_send, o_recv, s_send, s_recv,
):
    n_pipe, n_ctx, n_head = sizes
    tokens, width = x_hbm.shape
    pieces, chunks = width // LANES, tokens // CHUNK
    heads = ratev.shape[1]
    share = tokens // n_head
    sec, blk, me = lax.axis_index("pipe"), lax.axis_index("ctx"), lax.axis_index("head")
    dest_sec = lax.rem(sec + 1, n_pipe)

    def ctx_of(step):
        return {"ctx": lax.rem(blk + n_ctx + step, n_ctx)}

    barrier = pltpu.get_barrier_semaphore()
    for step in range(1, n_ctx):
        pl.semaphore_signal(barrier, inc=1, device_id=ctx_of(step), device_id_type=MESH)
    for h in range(n_head):
        pl.semaphore_signal(
            barrier, inc=1, device_id={"pipe": lax.rem(sec + n_pipe - 1, n_pipe), "head": h}, device_id_type=MESH
        )

    smalls = [
        pltpu.make_async_copy(src, dst, small_sem.at[n])
        for n, (src, dst) in enumerate((
            (seg_hbm, segv), (dt_hbm, dtv), (bias_hbm, biasv), (rate_hbm, ratev), (convbc_hbm, conv_bc),
            (convx_hbm, conv_x), (skip_hbm, skipv), (gain_hbm, gainv),
        ))
    ]
    for copy in smalls[:5]:
        copy.start()
    load_b = pltpu.make_async_copy(b_hbm, bv, load_sem.at[pieces])
    load_c = pltpu.make_async_copy(c_hbm, cv, load_sem.at[pieces + 1])
    load_z = pltpu.make_async_copy(z_hbm, zv, load_sem.at[pieces + 2])
    load_b.start()
    for copy in smalls[5:]:
        copy.start()
    for p in range(pieces):
        pltpu.make_async_copy(x_hbm.at[:, pl.ds(p * LANES, LANES)], xv.at[p], load_sem.at[p]).start()
    load_c.start()
    load_z.start()
    def remote(src, dst, send, recv, device):
        return pltpu.make_async_remote_copy(
            src_ref=src, dst_ref=dst, send_sem=send, recv_sem=recv, device_id=device, device_id_type=MESH
        )

    tail_rows = pl.ds(tokens - MARGIN, MARGIN)
    margins = [
        remote(seg_hbm.at[:, pl.ds(tokens - LANES, LANES)], mseg, marg_send.at[0], marg_recv.at[0], ctx_of(1)),
        remote(b_hbm.at[tail_rows, :], mb, marg_send.at[1], marg_recv.at[1], ctx_of(1)),
        remote(x_hbm.at[tail_rows, :], mx, marg_send.at[2], marg_recv.at[2], ctx_of(1)),
        remote(c_hbm.at[tail_rows, :], mc, marg_send.at[3], marg_recv.at[3], ctx_of(1)),
    ]

    def margin(n):
        @pl.when(blk > 0)
        def _():
            margins[n].wait_recv()

    def state_copies(p, k):
        owner = {"ctx": 2 * p + k}
        return (
            remote(loc_out.at[p, k], loc_in.at[blk], l_send.at[p, k], l_recv.at[blk], owner),
            remote(t_out.at[p], t_in.at[blk], t_send.at[p, k], t_recv.at[blk], owner),
        )

    def state_waits(block):
        return (
            remote(loc_out.at[0, 0], loc_in.at[block], l_send.at[0, 0], l_recv.at[block], ctx_of(1)),
            remote(t_out.at[0], t_in.at[block], t_send.at[0, 0], t_recv.at[block], ctx_of(1)),
        )

    def carry_copy(block):
        return remote(
            c_out.at[block], c_in.at[blk // 2, lax.rem(blk, 2)], c_send.at[block], c_recv.at[blk // 2, lax.rem(blk, 2)],
            {"ctx": block},
        )

    def carry_wait(p, k):
        return remote(c_out.at[0], c_in.at[p, k], c_send.at[0], c_recv.at[p, k], ctx_of(1))

    def row_copy(p, d):
        return remote(
            sendbuf.at[p, pl.ds(d * share, share), :],
            recvbuf.at[me, p],
            o_send.at[d, p],
            o_recv.at[me, p],
            {"pipe": dest_sec, "head": d},
        )

    def row_wait(p, h):
        remote(
            sendbuf.at[p, pl.ds(0, share), :], recvbuf.at[h, p], o_send.at[0, p], o_recv.at[h, p],
            {"pipe": dest_sec, "head": 0},
        ).wait_recv()

    def scale_copy(d):
        return remote(scale_out.at[d], scale_in.at[me], s_send.at[d], s_recv.at[me], {"pipe": dest_sec, "head": d})

    def scale_wait(h):
        remote(
            scale_out.at[0], scale_in.at[h], s_send.at[0], s_recv.at[h], {"pipe": dest_sec, "head": 0}
        ).wait_recv()

    row_at = lax.broadcasted_iota(jnp.int32, (4 * heads, width), 0)
    lane_at = lax.broadcasted_iota(jnp.int32, (4 * heads, width), 1)
    mine = lax.rem(row_at, heads) == lane_at // (width // heads)
    inner_rows = mine & (row_at < 2 * heads)
    outer_rows = mine & (row_at >= 2 * heads)
    for p in range(pieces):
        lanes = slice(p * LANES, (p + 1) * LANES)
        spread_in[:, lanes] = inner_rows[:, lanes].astype(BF16)
        spread_out[:, lanes] = outer_rows[:, lanes].astype(BF16)

    @pl.when(blk == 0)
    def _():
        mx[...] = jnp.zeros_like(mx)
        mb[...] = jnp.zeros_like(mb)
        mc[...] = jnp.zeros_like(mc)
        mseg[...] = jnp.full_like(mseg, -1)

    for copy in smalls[:4]:
        copy.wait()
    eye = lax.broadcasted_iota(jnp.int32, (heads, heads), 0) == lax.broadcasted_iota(jnp.int32, (heads, heads), 1)
    bias = jnp.sum(jnp.where(eye, biasv[...], 0.0), axis=1, keepdims=True)
    rate = jnp.sum(jnp.where(eye, ratev[...], 0.0), axis=1, keepdims=True)
    raw = dtv[...] + bias
    steps = jnp.maximum(raw, 0.0) + jnp.log1p(jnp.exp(-jnp.abs(raw)))
    decay = -steps * rate
    high, rest = halves(decay)
    mid, low = halves(decay - high.astype(F32))
    split = jnp.concatenate([high, mid, low], axis=0)
    at = lax.broadcasted_iota(jnp.int32, (CHUNK, CHUNK), 0)
    of = lax.broadcasted_iota(jnp.int32, (CHUNK, CHUNK), 1)
    upper = (at <= of).astype(BF16)
    unit = (at == of).astype(BF16)
    for j in range(chunks):
        sums = nn(split[:, j * CHUNK : (j + 1) * CHUNK], upper)
        cum = sums[:heads] + sums[heads : 2 * heads] + sums[2 * heads :]
        in_high, in_low = halves(jnp.exp(-cum) * steps[:, j * CHUNK : (j + 1) * CHUNK])
        out_high, out_low = halves(jnp.exp(cum))
        both = jnp.concatenate([in_high, in_low, out_high, out_low], axis=0)
        fac[pl.ds(j * CHUNK, CHUNK), :] = nt(unit, both).astype(BF16)

    for n in range(tokens // LANES):
        segc[pl.ds(MARGIN + n * LANES, LANES), :] = column(segv[:, pl.ds(n * LANES, LANES)].astype(F32))

    pl.semaphore_wait(barrier, n_ctx - 1 + n_head)

    @pl.when(blk < n_ctx - 1)
    def _():
        for copy in margins:
            copy.start()

    def taps_of(r, size):
        here = segc[pl.ds(MARGIN + r, size), :]
        for j in range(1, 4):
            same = segc[pl.ds(MARGIN + r - j, size), :] == here
            taps[j - 1, pl.ds(r, size), :] = same.astype(F32)

    def conv_rows(w, r, size):
        total = w[3:4, :] * ext[pl.ds(MARGIN + r, size), :]
        for j in range(1, 4):
            shifted = ext[pl.ds(MARGIN + r - j, size), :]
            total = total + (w[3 - j : 4 - j, :] * shifted) * taps[j - 1, pl.ds(r, size), :]
        return silu(total)

    part = 64
    for copy in smalls[4:]:
        copy.wait()
    load_b.wait()
    ext[pl.ds(MARGIN, tokens), :] = bv[...].astype(F32)
    for r in range(part, tokens, part):
        taps_of(r, part)
        bv[pl.ds(r, part), :] = conv_rows(conv_bc[0], r, part).astype(BF16)
    margin(0)
    segc[pl.ds(0, MARGIN), :] = column(mseg[...].astype(F32))[LANES - MARGIN :, :]
    prior = segc[pl.ds(MARGIN - 1, 1), :]
    lasts = [segc[pl.ds(MARGIN + (j + 1) * CHUNK - 1, 1), :] for j in range(chunks)]
    taps_of(0, part)
    for r in range(0, tokens, LANES):
        taps[3, pl.ds(r, LANES), :] = (segc[pl.ds(MARGIN + r, LANES), :] == prior).astype(F32)
    margin(1)
    ext[pl.ds(0, MARGIN), :] = mb[...].astype(F32)
    bv[pl.ds(0, part), :] = conv_rows(conv_bc[0], 0, part).astype(BF16)
    for j in range(chunks):
        seg_t = segc[pl.ds(MARGIN + j * CHUNK, CHUNK), :]
        kept = jnp.where(seg_t == lasts[j], bv[pl.ds(j * CHUNK, CHUNK), :].astype(F32), 0.0)
        bmt[j] = kept.T.astype(BF16)

    def wide(row):
        return jnp.concatenate([row] * pieces, axis=1)

    rows = []
    for j in range(chunks):
        ends = nn(fac[pl.ds((j + 1) * CHUNK - 16, 16), :], spread_out[...])[15:16, :]
        rows.append(ends)
        if j > 0:
            rows.append(jnp.where(wide((lasts[j] == lasts[j - 1]).astype(F32)) > 0.5, ends, 0.0))
    total = rows[0] * rows[1] * rows[3]
    rows.append(jnp.where(wide((lasts[-1] == prior).astype(F32)) > 0.5, total, 0.0))
    skip_high, skip_low = halves(skipv[...])
    nothing = jnp.zeros((1, 2 * heads), BF16)
    skips = jnp.concatenate([nothing, skip_high, skip_low], axis=1)
    skips = jnp.concatenate([skips, jnp.zeros((15, 4 * heads), BF16)], axis=0)
    rows.append(nn(skips, spread_out[...])[0:1, :])
    rows.append(jnp.zeros((8 - len(rows), width), F32))
    rows_s[...] = jnp.concatenate(rows, axis=0)

    margin(2)

    def turned(step):
        away = (step + 1) // 2
        return lax.rem(blk // 2 + jnp.where(lax.rem(step, 2) == 1, away, pieces - away), pieces)

    @pl.loop(0, pieces)
    def _(turn):
        p = turned(pieces - 1 - turn)
        lanes = pl.ds(pl.multiple_of(p * LANES, LANES), LANES)
        pltpu.make_async_copy(x_hbm.at[:, lanes], xv.at[p], load_sem.at[p]).wait()
        ext[pl.ds(0, MARGIN), :] = mx[:, lanes].astype(F32)
        ext[pl.ds(MARGIN, tokens), :] = xv[p].astype(F32)
        w = conv_x[:, lanes]
        spread = spread_in[:, lanes]
        factors = rows_s[:, lanes]
        state, row = None, 0
        for j in range(chunks):
            for r in range(j * CHUNK, (j + 1) * CHUNK, part):
                span = pl.ds(r, part)
                value = conv_rows(w, r, part).astype(BF16)
                xs[p, span, :] = value
                xsc[p, span, :] = (value.astype(F32) * nn(fac[span, :], spread)).astype(BF16)
            own = nn(bmt[j], xsc[p, pl.ds(j * CHUNK, CHUNK), :])
            if j == 0:
                state = factors[row : row + 1, :] * own
                row += 1
            else:
                hid[p, j - 1] = state.astype(BF16)
                state = factors[row + 1 : row + 2, :] * state + factors[row : row + 1, :] * own
                row += 2
        through = factors[row : row + 1, :]

        for k in range(2):
            loc_out[p, k] = state[k * HALF : (k + 1) * HALF, :].astype(BF16)
        t_out[p] = through

        for k in range(2):
            owner = 2 * p + k

            @pl.when((blk < n_ctx - 1) & (owner != blk))
            def _():
                for copy in state_copies(p, k):
                    copy.start()

            @pl.when((blk < n_ctx - 1) & (owner == blk))
            def _():
                loc_in[blk] = state[k * HALF : (k + 1) * HALF, :].astype(BF16)
                t_in[blk] = through

    load_c.wait()
    margin(3)
    ext[pl.ds(0, MARGIN), :] = mc[...].astype(F32)
    ext[pl.ds(MARGIN, tokens), :] = cv[...].astype(F32)
    for r in range(0, tokens, part):
        cs[pl.ds(r, part), :] = conv_rows(conv_bc[1], r, part).astype(BF16)
    for j in range(chunks):
        span = pl.ds(j * CHUNK, CHUNK)
        seg_t = segc[pl.ds(MARGIN + j * CHUNK, CHUNK), :]
        for first in range(0, CHUNK, LANES):
            seg_u = segv[:, pl.ds(j * CHUNK + first, LANES)].astype(F32)
            score = nt(cs[span, :], bv[pl.ds(j * CHUNK + first, LANES), :])
            keep = (seg_t == seg_u) & (at[:, :LANES] >= of[:, :LANES] + first)
            smask[j, :, pl.ds(first, LANES)] = jnp.where(keep, score, 0.0).astype(BF16)
        if j > 0:
            kept = jnp.where(seg_t == lasts[j - 1], cs[span, :].astype(F32), 0.0)
            cmask[j - 1] = kept.astype(BF16)
    load_z.wait()

    ssq[...] = jnp.zeros_like(ssq)
    scale_out[...] = jnp.zeros_like(scale_out)

    @pl.loop(0, pieces)
    def _(p):
        lanes = pl.ds(pl.multiple_of(p * LANES, LANES), LANES)
        factors = rows_s[:, lanes]
        skip = factors[2 * chunks : 2 * chunks + 1, :]
        spread = spread_out[:, lanes]
        before = None
        for j in range(chunks):
            inner = nn(smask[j], xsc[p, pl.ds(j * CHUNK, CHUNK), :])
            if j > 0:
                inner = inner + nn(cmask[j - 1], hid[p, j - 1])
                end = factors[0:1, :] if j == 1 else factors[2 * j - 3 : 2 * j - 2, :]
                before = end if before is None else before * end
            for r in range(0, CHUNK, part):
                span = pl.ds(j * CHUNK + r, part)
                gate = silu(zv[span, lanes].astype(F32))
                grown = nn(fac[span, :], spread)
                mixed = grown * inner[r : r + part, :] + skip * xs[p, span, :].astype(F32)
                yg[p, span, :] = mixed * gate
                entry = grown * taps[3, span, :]
                if before is not None:
                    entry = entry * before
                eg[p, span, :] = entry * gate

    scan_s[...] = jnp.zeros_like(scan_s)

    @pl.loop(0, n_ctx - 1)
    def _(block):
        @pl.when(block != blk)
        def _():
            for copy in state_waits(block):
                copy.wait_recv()

        value = t_in[block] * scan_s[...] + loc_in[block].astype(F32)
        scan_s[...] = value
        c_out[block + 1] = value.astype(BF16)

        @pl.when(block + 1 != blk)
        def _():
            carry_copy(block + 1).start()

        @pl.when(block + 1 == blk)
        def _():
            c_in[blk // 2, lax.rem(blk, 2)] = value.astype(BF16)

    @pl.loop(0, pieces)
    def _(turn):
        p = turned(turn)
        lanes = pl.ds(pl.multiple_of(p * LANES, LANES), LANES)

        @pl.when(blk == 0)
        def _():
            car[...] = jnp.zeros_like(car)

        for k in range(2):

            @pl.when((blk > 0) & (2 * p + k != blk))
            def _():
                carry_wait(p, k).wait_recv()

            @pl.when(blk > 0)
            def _():
                car[pl.ds(k * HALF, HALF), :] = c_in[p, k]

        gain = gainv[:, lanes]
        state = car[...]
        for r in range(0, tokens, part):
            span = pl.ds(r, part)
            gated = yg[p, span, :] + eg[p, span, :] * nn(cs[span, :], state)
            ssq[span, :] += gated * gated
            sendbuf[p, span, :] = (gated * gain).astype(BF16)
        for other in range(n_head):
            row_copy(p, lax.rem(me + other, n_head)).start()

    for d in range(n_head):
        for n, first in enumerate((0, share - LANES)):
            total = jnp.sum(ssq[pl.ds(d * share + first, LANES), :].T, axis=0, keepdims=True)
            scale_out[d, pl.ds(n, 1), :] = lax.rsqrt(total * (1.0 / width) + 1e-05)
        scale_copy(d).start()

    @pl.loop(0, pieces)
    def _(p):
        for k in range(2):

            @pl.when((blk < n_ctx - 1) & (2 * p + k != blk))
            def _():
                for copy in state_copies(p, k):
                    copy.wait_send()

    @pl.loop(1, n_ctx)
    def _(block):
        @pl.when(block != blk)
        def _():
            carry_copy(block).wait_send()

    @pl.when(blk < n_ctx - 1)
    def _():
        for copy in margins:
            copy.wait_send()

    @pl.loop(0, pieces)
    def _(p):
        for h in range(n_head):
            row_copy(p, h).wait_send()
            row_wait(p, h)

    for h in range(n_head):
        scale_copy(h).wait_send()
        scale_wait(h)


def scaled(rows_hbm, scale_hbm, out_hbm, rows_v, scale_v, out_v, in_sem, out_sem):
    groups, pieces, share, _ = rows_v.shape
    width = pieces * LANES
    scales = pltpu.make_async_copy(scale_hbm, scale_v, in_sem.at[groups])
    scales.start()
    loads = [pltpu.make_async_copy(rows_hbm.at[g], rows_v.at[g], in_sem.at[g]) for g in range(groups)]
    stores = [
        pltpu.make_async_copy(
            out_v.at[:, pl.ds(g * width, width)], out_hbm.at[:, pl.ds(g * width, width)], out_sem.at[g]
        )
        for g in range(groups)
    ]
    for copy in loads:
        copy.start()
    scales.wait()
    rest = pl.ds(LANES, share - LANES)
    for g in range(groups):
        first = column(scale_v[g, pl.ds(0, 1), :])
        second = column(scale_v[g, pl.ds(1, 1), :])[2 * LANES - share :, :]
        loads[g].wait()
        for p in range(pieces):
            lanes = pl.ds(g * width + p * LANES, LANES)
            out_v[pl.ds(0, LANES), lanes] = (rows_v[g, p, pl.ds(0, LANES), :].astype(F32) * first).astype(BF16)
            out_v[rest, lanes] = (rows_v[g, p, rest, :].astype(F32) * second).astype(BF16)
        stores[g].start()
    for copy in stores:
        copy.wait()


def solution(mesh):
    sizes = tuple(mesh.shape[name] for name in ("pipe", "ctx", "head"))
    n_ctx, n_head = sizes[1:]

    def shards(
        x_in, b_in, c_in, z_in, dt_raw, seg_ids, conv_x, conv_bc, decay_rate, dt_bias, skip_d, norm_gain
    ):
        _, tokens, width = x_in.shape
        state = b_in.shape[2]
        heads = decay_rate.shape[1]
        pieces, chunks, share = width // LANES, tokens // CHUNK, tokens // n_head
        vmem, sem = pltpu.VMEM, pltpu.SemaphoreType.DMA
        scratch = [
            vmem((pieces, tokens, LANES), BF16),
            vmem((tokens, state), BF16),
            vmem((tokens, state), BF16),
            vmem((tokens, width), BF16),
            vmem((heads, tokens), F32),
            vmem((1, tokens), jnp.int32),
            vmem((4, width), F32),
            vmem((2, 4, state), F32),
            vmem((1, heads), F32),
            vmem((1, heads), F32),
            vmem((1, heads), F32),
            vmem((1, width), F32),
            vmem((MARGIN, width), BF16),
            vmem((MARGIN, state), BF16),
            vmem((MARGIN, state), BF16),
            vmem((1, LANES), jnp.int32),
            vmem((MARGIN + tokens, LANES), F32),
            vmem((MARGIN + tokens, LANES), F32),
            vmem((4, tokens, LANES), F32),
            vmem((tokens, 4 * heads), BF16),
            vmem((4 * heads, width), BF16),
            vmem((4 * heads, width), BF16),
            vmem((8, width), F32),
            vmem((chunks, state, CHUNK), BF16),
            vmem((chunks, CHUNK, CHUNK), BF16),
            vmem((tokens, state), BF16),
            vmem((chunks - 1, CHUNK, state), BF16),
            vmem((pieces, tokens, LANES), BF16),
            vmem((pieces, tokens, LANES), BF16),
            vmem((pieces, chunks - 1, state, LANES), BF16),
            vmem((pieces, tokens, LANES), F32),
            vmem((pieces, tokens, LANES), F32),
            vmem((tokens, LANES), F32),
            vmem((pieces, 2, HALF, LANES), BF16),
            vmem((pieces, 1, LANES), F32),
            vmem((n_ctx, HALF, LANES), BF16),
            vmem((n_ctx, 1, LANES), F32),
            vmem((HALF, LANES), F32),
            vmem((n_ctx, HALF, LANES), BF16),
            vmem((pieces, 2, HALF, LANES), BF16),
            vmem((state, LANES), BF16),
            vmem((pieces, tokens, LANES), BF16),
            vmem((n_head, 8, LANES), F32),
            sem((pieces + 3,)), sem((8,)),
            sem((4,)), sem((4,)),
            sem((pieces, 2)), sem((n_ctx,)),
            sem((pieces, 2)), sem((n_ctx,)),
            sem((n_ctx,)), sem((pieces, 2)),
            sem((n_head, pieces)), sem((n_head, pieces)),
            sem((n_head,)), sem((n_head,)),
        ]
        anywhere = pl.BlockSpec(memory_space=pl.ANY)
        rows, scales = pl.pallas_call(
            functools.partial(kernel, sizes),
            out_shape=(
                jax.ShapeDtypeStruct((n_head, pieces, share, LANES), BF16),
                jax.ShapeDtypeStruct((n_head, 8, LANES), F32),
            ),
            in_specs=[anywhere] * 12,
            out_specs=(anywhere, anywhere),
            scratch_shapes=scratch,
            compiler_params=pltpu.CompilerParams(collective_id=0, has_side_effects=True),
        )(
            x_in[0], b_in[0], c_in[0], z_in[0], dt_raw[0].T, seg_ids, conv_x[0], conv_bc[0],
            decay_rate, dt_bias, skip_d, norm_gain,
        )
        rows = pl.pallas_call(
            scaled,
            out_shape=jax.ShapeDtypeStruct((share, n_head * width), BF16),
            in_specs=[anywhere, anywhere],
            out_specs=anywhere,
            scratch_shapes=[
                vmem((n_head, pieces, share, LANES), BF16),
                vmem((n_head, 8, LANES), F32),
                vmem((share, n_head * width), BF16),
                sem((n_head + 1,)),
                sem((n_head,)),
            ],
        )(rows, scales)
        return rows[None]

    placed = (
        P("pipe", "ctx", "head"),
        P("pipe", "ctx", "head"),
        P("pipe", "ctx", "head"),
        P("pipe", "ctx", "head"),
        P("pipe", "ctx", "head"),
        P("pipe", "ctx"),
        P("pipe", None, "head"),
        P("pipe", None, None, "head"),
        P("pipe", "head"),
        P("pipe", "head"),
        P("pipe", "head"),
        P("pipe", "head"),
    )
    return jax.shard_map(
        shards,
        mesh=mesh,
        in_specs=placed,
        out_specs=P("pipe", ("ctx", "head"), None),
        check_vma=False,
    )
```

```python
import functools

import jax
import jax.numpy as jnp
from jax import lax
from jax.experimental import pallas as pl
from jax.experimental.pallas import tpu as pltpu
from jax.sharding import PartitionSpec as P

F32 = jnp.float32
BF16 = jnp.bfloat16
MESH = pl.DeviceIdType.MESH
CHUNK = 256
LANES = 128
MARGIN = 16
EARLY = 5
HALF = 64


def nt(a, b, **kw):
    return lax.dot_general(a, b, (((1,), (1,)), ((), ())), preferred_element_type=F32, **kw)


def nn(a, b, **kw):
    return lax.dot_general(a, b, (((1,), (0,)), ((), ())), preferred_element_type=F32, **kw)


def halves(a):
    high = a.astype(BF16)
    return high, (a - high.astype(F32)).astype(BF16)


def silu(a):
    half = 0.5 * a
    return half + half * jnp.tanh(half)


def column(row):
    return jnp.broadcast_to(row, (LANES, LANES)).T


def kernel(
    sizes,
    x_hbm, b_hbm, c_hbm, z_hbm, dt_hbm, seg_hbm, convx_hbm, convbc_hbm, rate_hbm, bias_hbm, skip_hbm, gain_hbm,
    recvbuf, scale_in,
    xv, bv, cv, zv, dtv, segv, conv_x, conv_bc, ratev, biasv, skipv, gainv, mx, mb, mc, mseg,
    ext, segc, taps, fac, spread_in, spread_out, rows_s, bmt, smask, cs, cmask,
    xs, xsc, hid, yg, eg, ssq, loc_out, t_out, loc_in, t_in, scan_s, c_out, c_in, car, sendbuf, scale_out,
    load_sem, small_sem, marg_send, marg_recv, l_send, l_recv, t_send, t_recv, c_send, c_recv,
    o_send, o_recv, s_send, s_recv,
):
    n_pipe, n_ctx, n_head = sizes
    tokens, width = x_hbm.shape
    pieces, chunks = width // LANES, tokens // CHUNK
    heads = ratev.shape[1]
    share = tokens // n_head
    sec, blk, me = lax.axis_index("pipe"), lax.axis_index("ctx"), lax.axis_index("head")
    dest_sec = lax.rem(sec + 1, n_pipe)

    def ctx_of(step):
        return {"ctx": lax.rem(blk + n_ctx + step, n_ctx)}

    barrier = pltpu.get_barrier_semaphore()
    for step in range(1, n_ctx):
        pl.semaphore_signal(barrier, inc=1, device_id=ctx_of(step), device_id_type=MESH)
    for h in range(n_head):
        pl.semaphore_signal(
            barrier, inc=1, device_id={"pipe": lax.rem(sec + n_pipe - 1, n_pipe), "head": h}, device_id_type=MESH
        )

    smalls = [
        pltpu.make_async_copy(src, dst, small_sem.at[n])
        for n, (src, dst) in enumerate((
            (seg_hbm, segv), (dt_hbm, dtv), (bias_hbm, biasv), (rate_hbm, ratev), (convbc_hbm, conv_bc),
            (convx_hbm, conv_x), (skip_hbm, skipv), (gain_hbm, gainv),
        ))
    ]
    for copy in smalls[:5]:
        copy.start()
    load_b = pltpu.make_async_copy(b_hbm, bv, load_sem.at[pieces])
    load_c = pltpu.make_async_copy(c_hbm, cv, load_sem.at[pieces + 1])
    load_z = pltpu.make_async_copy(z_hbm, zv, load_sem.at[pieces + 2])
    load_b.start()
    for copy in smalls[5:]:
        copy.start()
    for p in range(pieces):
        pltpu.make_async_copy(x_hbm.at[:, pl.ds(p * LANES, LANES)], xv.at[p], load_sem.at[p]).start()
    load_c.start()
    load_z.start()
    def remote(src, dst, send, recv, device):
        return pltpu.make_async_remote_copy(
            src_ref=src, dst_ref=dst, send_sem=send, recv_sem=recv, device_id=device, device_id_type=MESH
        )

    tail_rows = pl.ds(tokens - MARGIN, MARGIN)
    margins = [
        remote(seg_hbm.at[:, pl.ds(tokens - LANES, LANES)], mseg, marg_send.at[0], marg_recv.at[0], ctx_of(1)),
        remote(b_hbm.at[tail_rows, :], mb, marg_send.at[1], marg_recv.at[1], ctx_of(1)),
        remote(x_hbm.at[tail_rows, :], mx, marg_send.at[2], marg_recv.at[2], ctx_of(1)),
        remote(c_hbm.at[tail_rows, :], mc, marg_send.at[3], marg_recv.at[3], ctx_of(1)),
    ]

    def margin(n):
        @pl.when(blk > 0)
        def _():
            margins[n].wait_recv()

    def state_copies(p, k):
        owner = {"ctx": 2 * p + k}
        return (
            remote(loc_out.at[p, k], loc_in.at[blk], l_send.at[p, k], l_recv.at[blk], owner),
            remote(t_out.at[p], t_in.at[blk], t_send.at[p, k], t_recv.at[blk], owner),
        )

    def state_waits(block):
        return (
            remote(loc_out.at[0, 0], loc_in.at[block], l_send.at[0, 0], l_recv.at[block], ctx_of(1)),
            remote(t_out.at[0], t_in.at[block], t_send.at[0, 0], t_recv.at[block], ctx_of(1)),
        )

    def carry_copy(block):
        return remote(
            c_out.at[block], c_in.at[blk // 2, lax.rem(blk, 2)], c_send.at[block], c_recv.at[blk // 2, lax.rem(blk, 2)],
            {"ctx": block},
        )

    def carry_wait(p, k):
        return remote(c_out.at[0], c_in.at[p, k], c_send.at[0], c_recv.at[p, k], ctx_of(1))

    def row_copy(p, d):
        return remote(
            sendbuf.at[p, pl.ds(d * share, share), :],
            recvbuf.at[me, p],
            o_send.at[d, p],
            o_recv.at[me, p],
            {"pipe": dest_sec, "head": d},
        )

    def row_wait(p, h):
        remote(
            sendbuf.at[p, pl.ds(0, share), :], recvbuf.at[h, p], o_send.at[0, p], o_recv.at[h, p],
            {"pipe": dest_sec, "head": 0},
        ).wait_recv()

    def scale_copy(d):
        return remote(scale_out.at[d], scale_in.at[me], s_send.at[d], s_recv.at[me], {"pipe": dest_sec, "head": d})

    def scale_wait(h):
        remote(
            scale_out.at[0], scale_in.at[h], s_send.at[0], s_recv.at[h], {"pipe": dest_sec, "head": 0}
        ).wait_recv()

    row_at = lax.broadcasted_iota(jnp.int32, (4 * heads, width), 0)
    lane_at = lax.broadcasted_iota(jnp.int32, (4 * heads, width), 1)
    mine = lax.rem(row_at, heads) == lane_at // (width // heads)
    inner_rows = mine & (row_at < 2 * heads)
    outer_rows = mine & (row_at >= 2 * heads)
    for p in range(pieces):
        lanes = slice(p * LANES, (p + 1) * LANES)
        spread_in[:, lanes] = inner_rows[:, lanes].astype(BF16)
        spread_out[:, lanes] = outer_rows[:, lanes].astype(BF16)

    @pl.when(blk == 0)
    def _():
        mx[...] = jnp.zeros_like(mx)
        mb[...] = jnp.zeros_like(mb)
        mc[...] = jnp.zeros_like(mc)
        mseg[...] = jnp.full_like(mseg, -1)

    for copy in smalls[:4]:
        copy.wait()
    eye = lax.broadcasted_iota(jnp.int32, (heads, heads), 0) == lax.broadcasted_iota(jnp.int32, (heads, heads), 1)
    bias = jnp.sum(jnp.where(eye, biasv[...], 0.0), axis=1, keepdims=True)
    rate = jnp.sum(jnp.where(eye, ratev[...], 0.0), axis=1, keepdims=True)
    raw = dtv[...] + bias
    steps = jnp.maximum(raw, 0.0) + jnp.log1p(jnp.exp(-jnp.abs(raw)))
    decay = -steps * rate
    high, rest = halves(decay)
    mid, low = halves(decay - high.astype(F32))
    split = jnp.concatenate([high, mid, low], axis=0)
    at = lax.broadcasted_iota(jnp.int32, (CHUNK, CHUNK), 0)
    of = lax.broadcasted_iota(jnp.int32, (CHUNK, CHUNK), 1)
    upper = (at <= of).astype(BF16)
    unit = (at == of).astype(BF16)
    for j in range(chunks):
        sums = nn(split[:, j * CHUNK : (j + 1) * CHUNK], upper)
        cum = sums[:heads] + sums[heads : 2 * heads] + sums[2 * heads :]
        in_high, in_low = halves(jnp.exp(-cum) * steps[:, j * CHUNK : (j + 1) * CHUNK])
        out_high, out_low = halves(jnp.exp(cum))
        both = jnp.concatenate([in_high, in_low, out_high, out_low], axis=0)
        fac[pl.ds(j * CHUNK, CHUNK), :] = nt(unit, both).astype(BF16)

    for n in range(tokens // LANES):
        segc[pl.ds(MARGIN + n * LANES, LANES), :] = column(segv[:, pl.ds(n * LANES, LANES)].astype(F32))

    pl.semaphore_wait(barrier, n_ctx - 1 + n_head)

    @pl.when(blk < n_ctx - 1)
    def _():
        for copy in margins:
            copy.start()

    def taps_of(r, size):
        here = segc[pl.ds(MARGIN + r, size), :]
        for j in range(1, 4):
            same = segc[pl.ds(MARGIN + r - j, size), :] == here
            taps[j - 1, pl.ds(r, size), :] = same.astype(F32)

    def conv_rows(w, r, size):
        total = w[3:4, :] * ext[pl.ds(MARGIN + r, size), :]
        for j in range(1, 4):
            shifted = ext[pl.ds(MARGIN + r - j, size), :]
            total = total + (w[3 - j : 4 - j, :] * shifted) * taps[j - 1, pl.ds(r, size), :]
        return silu(total)

    part = 64
    for copy in smalls[4:]:
        copy.wait()
    load_b.wait()
    ext[pl.ds(MARGIN, tokens), :] = bv[...].astype(F32)
    for r in range(part, tokens, part):
        taps_of(r, part)
        bv[pl.ds(r, part), :] = conv_rows(conv_bc[0], r, part).astype(BF16)
    margin(0)
    segc[pl.ds(0, MARGIN), :] = column(mseg[...].astype(F32))[LANES - MARGIN :, :]
    prior = segc[pl.ds(MARGIN - 1, 1), :]
    lasts = [segc[pl.ds(MARGIN + (j + 1) * CHUNK - 1, 1), :] for j in range(chunks)]
    taps_of(0, part)
    for r in range(0, tokens, LANES):
        taps[3, pl.ds(r, LANES), :] = (segc[pl.ds(MARGIN + r, LANES), :] == prior).astype(F32)
    margin(1)
    ext[pl.ds(0, MARGIN), :] = mb[...].astype(F32)
    bv[pl.ds(0, part), :] = conv_rows(conv_bc[0], 0, part).astype(BF16)
    for j in range(chunks):
        seg_t = segc[pl.ds(MARGIN + j * CHUNK, CHUNK), :]
        kept = jnp.where(seg_t == lasts[j], bv[pl.ds(j * CHUNK, CHUNK), :].astype(F32), 0.0)
        bmt[j] = kept.T.astype(BF16)

    def wide(row):
        return jnp.concatenate([row] * pieces, axis=1)

    rows = []
    for j in range(chunks):
        ends = nn(fac[pl.ds((j + 1) * CHUNK - 16, 16), :], spread_out[...])[15:16, :]
        rows.append(ends)
        if j > 0:
            rows.append(jnp.where(wide((lasts[j] == lasts[j - 1]).astype(F32)) > 0.5, ends, 0.0))
    total = rows[0] * rows[1] * rows[3]
    rows.append(jnp.where(wide((lasts[-1] == prior).astype(F32)) > 0.5, total, 0.0))
    skip_high, skip_low = halves(skipv[...])
    nothing = jnp.zeros((1, 2 * heads), BF16)
    skips = jnp.concatenate([nothing, skip_high, skip_low], axis=1)
    skips = jnp.concatenate([skips, jnp.zeros((15, 4 * heads), BF16)], axis=0)
    rows.append(nn(skips, spread_out[...])[0:1, :])
    rows.append(jnp.zeros((8 - len(rows), width), F32))
    rows_s[...] = jnp.concatenate(rows, axis=0)

    margin(2)

    def turned(step):
        away = (step + 1) // 2
        return lax.rem(blk // 2 + jnp.where(lax.rem(step, 2) == 1, away, pieces - away), pieces)

    @pl.loop(0, pieces)
    def _(turn):
        p = turned(pieces - 1 - turn)
        lanes = pl.ds(pl.multiple_of(p * LANES, LANES), LANES)
        pltpu.make_async_copy(x_hbm.at[:, lanes], xv.at[p], load_sem.at[p]).wait()
        ext[pl.ds(0, MARGIN), :] = mx[:, lanes].astype(F32)
        ext[pl.ds(MARGIN, tokens), :] = xv[p].astype(F32)
        w = conv_x[:, lanes]
        spread = spread_in[:, lanes]
        factors = rows_s[:, lanes]
        state, row = None, 0
        for j in range(chunks):
            for r in range(j * CHUNK, (j + 1) * CHUNK, part):
                span = pl.ds(r, part)
                value = conv_rows(w, r, part).astype(BF16)
                xs[p, span, :] = value
                xsc[p, span, :] = (value.astype(F32) * nn(fac[span, :], spread)).astype(BF16)
            own = nn(bmt[j], xsc[p, pl.ds(j * CHUNK, CHUNK), :])
            if j == 0:
                state = factors[row : row + 1, :] * own
                row += 1
            else:
                hid[p, j - 1] = state.astype(BF16)
                state = factors[row + 1 : row + 2, :] * state + factors[row : row + 1, :] * own
                row += 2
        through = factors[row : row + 1, :]

        for k in range(2):
            loc_out[p, k] = state[k * HALF : (k + 1) * HALF, :].astype(BF16)
        t_out[p] = through

        for k in range(2):
            owner = 2 * p + k

            @pl.when((blk < n_ctx - 1) & (owner != blk))
            def _():
                for copy in state_copies(p, k):
                    copy.start()

            @pl.when((blk < n_ctx - 1) & (owner == blk))
            def _():
                loc_in[blk] = state[k * HALF : (k + 1) * HALF, :].astype(BF16)
                t_in[blk] = through

    load_c.wait()
    margin(3)
    ext[pl.ds(0, MARGIN), :] = mc[...].astype(F32)
    ext[pl.ds(MARGIN, tokens), :] = cv[...].astype(F32)
    for r in range(0, tokens, part):
        cs[pl.ds(r, part), :] = conv_rows(conv_bc[1], r, part).astype(BF16)
    for j in range(chunks):
        span = pl.ds(j * CHUNK, CHUNK)
        seg_t = segc[pl.ds(MARGIN + j * CHUNK, CHUNK), :]
        for first in range(0, CHUNK, LANES):
            seg_u = segv[:, pl.ds(j * CHUNK + first, LANES)].astype(F32)
            score = nt(cs[span, :], bv[pl.ds(j * CHUNK + first, LANES), :])
            keep = (seg_t == seg_u) & (at[:, :LANES] >= of[:, :LANES] + first)
            smask[j, :, pl.ds(first, LANES)] = jnp.where(keep, score, 0.0).astype(BF16)
        if j > 0:
            kept = jnp.where(seg_t == lasts[j - 1], cs[span, :].astype(F32), 0.0)
            cmask[j - 1] = kept.astype(BF16)
    load_z.wait()

    ssq[...] = jnp.zeros_like(ssq)
    scale_out[...] = jnp.zeros_like(scale_out)

    @pl.loop(0, pieces)
    def _(p):
        lanes = pl.ds(pl.multiple_of(p * LANES, LANES), LANES)
        factors = rows_s[:, lanes]
        skip = factors[2 * chunks : 2 * chunks + 1, :]
        spread = spread_out[:, lanes]
        before = None
        for j in range(chunks):
            inner = nn(smask[j], xsc[p, pl.ds(j * CHUNK, CHUNK), :])
            if j > 0:
                inner = inner + nn(cmask[j - 1], hid[p, j - 1])
                end = factors[0:1, :] if j == 1 else factors[2 * j - 3 : 2 * j - 2, :]
                before = end if before is None else before * end
            for r in range(0, CHUNK, part):
                span = pl.ds(j * CHUNK + r, part)
                gate = silu(zv[span, lanes].astype(F32))
                grown = nn(fac[span, :], spread)
                mixed = grown * inner[r : r + part, :] + skip * xs[p, span, :].astype(F32)
                yg[p, span, :] = mixed * gate
                entry = grown * taps[3, span, :]
                if before is not None:
                    entry = entry * before
                eg[p, span, :] = entry * gate

    scan_s[...] = jnp.zeros_like(scan_s)

    @pl.loop(0, n_ctx - 1)
    def _(block):
        @pl.when(block != blk)
        def _():
            for copy in state_waits(block):
                copy.wait_recv()

        value = t_in[block] * scan_s[...] + loc_in[block].astype(F32)
        scan_s[...] = value
        c_out[block + 1] = value.astype(BF16)

        @pl.when((block + 1 <= EARLY) & (block + 1 != blk))
        def _():
            carry_copy(block + 1).start()

    @pl.when(blk > 0)
    def _():
        c_in[blk // 2, lax.rem(blk, 2)] = c_out[blk]

    @pl.loop(1, n_ctx)
    def _(step):
        away = (step + 1) // 2
        block = lax.rem(blk + jnp.where(lax.rem(step, 2) == 1, away, n_ctx - away), n_ctx)

        @pl.when(block > EARLY)
        def _():
            carry_copy(block).start()

    @pl.loop(0, pieces)
    def _(turn):
        p = turned(turn)
        lanes = pl.ds(pl.multiple_of(p * LANES, LANES), LANES)

        @pl.when(blk == 0)
        def _():
            car[...] = jnp.zeros_like(car)

        for k in range(2):

            @pl.when((blk > 0) & (2 * p + k != blk))
            def _():
                carry_wait(p, k).wait_recv()

            @pl.when(blk > 0)
            def _():
                car[pl.ds(k * HALF, HALF), :] = c_in[p, k]

        gain = gainv[:, lanes]
        state = car[...]
        for r in range(0, tokens, part):
            span = pl.ds(r, part)
            gated = yg[p, span, :] + eg[p, span, :] * nn(cs[span, :], state)
            ssq[span, :] += gated * gated
            sendbuf[p, span, :] = (gated * gain).astype(BF16)
        for other in range(n_head):
            row_copy(p, lax.rem(me + other, n_head)).start()

    for d in range(n_head):
        for n, first in enumerate((0, share - LANES)):
            total = jnp.sum(ssq[pl.ds(d * share + first, LANES), :].T, axis=0, keepdims=True)
            scale_out[d, pl.ds(n, 1), :] = lax.rsqrt(total * (1.0 / width) + 1e-05)
        scale_copy(d).start()

    @pl.loop(0, pieces)
    def _(p):
        for k in range(2):

            @pl.when((blk < n_ctx - 1) & (2 * p + k != blk))
            def _():
                for copy in state_copies(p, k):
                    copy.wait_send()

    @pl.loop(1, n_ctx)
    def _(block):
        @pl.when(block != blk)
        def _():
            carry_copy(block).wait_send()

    @pl.when(blk < n_ctx - 1)
    def _():
        for copy in margins:
            copy.wait_send()

    @pl.loop(0, pieces)
    def _(p):
        for h in range(n_head):
            row_copy(p, h).wait_send()
            row_wait(p, h)

    for h in range(n_head):
        scale_copy(h).wait_send()
        scale_wait(h)


def scaled(rows_hbm, scale_hbm, out_hbm, rows_v, scale_v, out_v, in_sem, out_sem):
    groups, pieces, share, _ = rows_v.shape
    width = pieces * LANES
    scales = pltpu.make_async_copy(scale_hbm, scale_v, in_sem.at[groups])
    scales.start()
    loads = [pltpu.make_async_copy(rows_hbm.at[g], rows_v.at[g], in_sem.at[g]) for g in range(groups)]
    stores = [
        pltpu.make_async_copy(
            out_v.at[:, pl.ds(g * width, width)], out_hbm.at[:, pl.ds(g * width, width)], out_sem.at[g]
        )
        for g in range(groups)
    ]
    for copy in loads:
        copy.start()
    scales.wait()
    rest = pl.ds(LANES, share - LANES)
    for g in range(groups):
        first = column(scale_v[g, pl.ds(0, 1), :])
        second = column(scale_v[g, pl.ds(1, 1), :])[2 * LANES - share :, :]
        loads[g].wait()
        for p in range(pieces):
            lanes = pl.ds(g * width + p * LANES, LANES)
            out_v[pl.ds(0, LANES), lanes] = (rows_v[g, p, pl.ds(0, LANES), :].astype(F32) * first).astype(BF16)
            out_v[rest, lanes] = (rows_v[g, p, rest, :].astype(F32) * second).astype(BF16)
        stores[g].start()
    for copy in stores:
        copy.wait()


def solution(mesh):
    sizes = tuple(mesh.shape[name] for name in ("pipe", "ctx", "head"))
    n_ctx, n_head = sizes[1:]

    def shards(
        x_in, b_in, c_in, z_in, dt_raw, seg_ids, conv_x, conv_bc, decay_rate, dt_bias, skip_d, norm_gain
    ):
        _, tokens, width = x_in.shape
        state = b_in.shape[2]
        heads = decay_rate.shape[1]
        pieces, chunks, share = width // LANES, tokens // CHUNK, tokens // n_head
        vmem, sem = pltpu.VMEM, pltpu.SemaphoreType.DMA
        scratch = [
            vmem((pieces, tokens, LANES), BF16),
            vmem((tokens, state), BF16),
            vmem((tokens, state), BF16),
            vmem((tokens, width), BF16),
            vmem((heads, tokens), F32),
            vmem((1, tokens), jnp.int32),
            vmem((4, width), F32),
            vmem((2, 4, state), F32),
            vmem((1, heads), F32),
            vmem((1, heads), F32),
            vmem((1, heads), F32),
            vmem((1, width), F32),
            vmem((MARGIN, width), BF16),
            vmem((MARGIN, state), BF16),
            vmem((MARGIN, state), BF16),
            vmem((1, LANES), jnp.int32),
            vmem((MARGIN + tokens, LANES), F32),
            vmem((MARGIN + tokens, LANES), F32),
            vmem((4, tokens, LANES), F32),
            vmem((tokens, 4 * heads), BF16),
            vmem((4 * heads, width), BF16),
            vmem((4 * heads, width), BF16),
            vmem((8, width), F32),
            vmem((chunks, state, CHUNK), BF16),
            vmem((chunks, CHUNK, CHUNK), BF16),
            vmem((tokens, state), BF16),
            vmem((chunks - 1, CHUNK, state), BF16),
            vmem((pieces, tokens, LANES), BF16),
            vmem((pieces, tokens, LANES), BF16),
            vmem((pieces, chunks - 1, state, LANES), BF16),
            vmem((pieces, tokens, LANES), F32),
            vmem((pieces, tokens, LANES), F32),
            vmem((tokens, LANES), F32),
            vmem((pieces, 2, HALF, LANES), BF16),
            vmem((pieces, 1, LANES), F32),
            vmem((n_ctx, HALF, LANES), BF16),
            vmem((n_ctx, 1, LANES), F32),
            vmem((HALF, LANES), F32),
            vmem((n_ctx, HALF, LANES), BF16),
            vmem((pieces, 2, HALF, LANES), BF16),
            vmem((state, LANES), BF16),
            vmem((pieces, tokens, LANES), BF16),
            vmem((n_head, 8, LANES), F32),
            sem((pieces + 3,)), sem((8,)),
            sem((4,)), sem((4,)),
            sem((pieces, 2)), sem((n_ctx,)),
            sem((pieces, 2)), sem((n_ctx,)),
            sem((n_ctx,)), sem((pieces, 2)),
            sem((n_head, pieces)), sem((n_head, pieces)),
            sem((n_head,)), sem((n_head,)),
        ]
        anywhere = pl.BlockSpec(memory_space=pl.ANY)
        rows, scales = pl.pallas_call(
            functools.partial(kernel, sizes),
            out_shape=(
                jax.ShapeDtypeStruct((n_head, pieces, share, LANES), BF16),
                jax.ShapeDtypeStruct((n_head, 8, LANES), F32),
            ),
            in_specs=[anywhere] * 12,
            out_specs=(anywhere, anywhere),
            scratch_shapes=scratch,
            compiler_params=pltpu.CompilerParams(collective_id=0, has_side_effects=True),
        )(
            x_in[0], b_in[0], c_in[0], z_in[0], dt_raw[0].T, seg_ids, conv_x[0], conv_bc[0],
            decay_rate, dt_bias, skip_d, norm_gain,
        )
        rows = pl.pallas_call(
            scaled,
            out_shape=jax.ShapeDtypeStruct((share, n_head * width), BF16),
            in_specs=[anywhere, anywhere],
            out_specs=anywhere,
            scratch_shapes=[
                vmem((n_head, pieces, share, LANES), BF16),
                vmem((n_head, 8, LANES), F32),
                vmem((share, n_head * width), BF16),
                sem((n_head + 1,)),
                sem((n_head,)),
            ],
        )(rows, scales)
        return rows[None]

    placed = (
        P("pipe", "ctx", "head"),
        P("pipe", "ctx", "head"),
        P("pipe", "ctx", "head"),
        P("pipe", "ctx", "head"),
        P("pipe", "ctx", "head"),
        P("pipe", "ctx"),
        P("pipe", None, "head"),
        P("pipe", None, None, "head"),
        P("pipe", "head"),
        P("pipe", "head"),
        P("pipe", "head"),
        P("pipe", "head"),
    )
    return jax.shard_map(
        shards,
        mesh=mesh,
        in_specs=placed,
        out_specs=P("pipe", ("ctx", "head"), None),
        check_vma=False,
    )
```
